32 devices in a mesh: xs: 4 (over y, x), ax: 8 (over z, core).
Axes of the slice: x: 2, y: 2, z: 4, core: 2. Of those that a mesh axis runs over, the one named last changes fastest.
Arguments:
- concentration: float32 [256, 128, 384], P('ax', 'xs'), may hold values from -4 to 4
- tissue_mask: int32 [256, 128, 384], P('ax', 'xs'), may hold values from 0 to 1
- wall_layer: int32 [256, 128, 384], P('ax', 'xs'), may hold values from 0 to 3, as said below
- stiffness: float32 [256, 128, 384], P('ax', 'xs'), may hold values from 1 to 2
- production: float32 [256, 128, 384], P('ax', 'xs'), may hold values from -3 to 3
- layer_diffusivity: float32 [4], replicated, may hold values from 1 to 2
- uptake_rate: float32 [4], replicated, may hold values from 0.1 to 0.5
Outputs:
- concentration_out: float32 [256, 128, 384], P('ax', 'xs')
The draws below stay inside these ranges and needn't reach their ends.
Inputs may be any that keep to these rules, and one draw needn't show every extreme that they name: `wall_layer`: indexes the tables of layer coefficients.
All inputs are finite; a program needn't handle non-finite values.
Results may differ from the reference program's by a relative error of at most 0.0003.
Values sent between devices are 32-bit elements; how exact they have to be, the bound alone decides.
A program may use at most 128 MiB of HBM per device.

```python
import math
import jax
import jax.numpy as jnp
from jax import lax

NY = 384
STEPS = 2
LAYERS = 4
NX = 128
NZ = 256
RZ = 3072


def wall_geometry(key):
    base_key = jax.random.fold_in(key, 11)
    subkeys = jax.random.split(base_key, 3)
    centre_x = NX // 2 + jax.random.randint(subkeys[0], (), -(NX // 8), NX // 8 + 1)
    centre_y = NY // 2 + jax.random.randint(subkeys[1], (), -(NY // 8), NY // 8 + 1)
    bulge_start = jax.random.randint(subkeys[2], (), 0, NZ - NZ // 4 + 1)
    lumen_radius = NX // 4
    bulge_size = max(NX // 16, 1)
    layer_width = max(NX // 16, 1)
    axial = jnp.arange(NZ, dtype=jnp.int32)[:, None, None]
    across = jnp.arange(NX, dtype=jnp.int32)[None, :, None]
    along_y = jnp.arange(NY, dtype=jnp.int32)[None, None, :]
    inside = ((axial >= bulge_start) & (axial < bulge_start + NZ // 4)).astype(jnp.int32)
    radius = lumen_radius + bulge_size * inside
    radial_sq = (across - centre_x) * (across - centre_x) + (along_y - centre_y) * (along_y - centre_y)
    return (radius, radial_sq, layer_width)


def draw_tissue_mask(key, part):
    radius, radial_sq, layer_width = wall_geometry(key)
    return (radial_sq >= radius * radius).astype(jnp.int32)


def draw_wall_layer(key, part):
    radius, radial_sq, layer_width = wall_geometry(key)
    labels = jnp.zeros(radial_sq.shape, jnp.int32)
    for band_index in range(1, 4):
        edge = radius + band_index * layer_width
        labels = labels + (radial_sq >= edge * edge).astype(jnp.int32)
    return labels


def draw_concentration(key, part):
    base_key = jax.random.fold_in(key, 23)
    return jnp.clip(jax.random.normal(base_key, (NZ, NX, NY), jnp.float32), -4.0, 4.0)


def block_scale(rng, extent, cuts, low, largest):
    factor_of = 1.0
    for axis_at, blocks in cuts:
        heights = jax.random.uniform(jax.random.fold_in(jax.random.fold_in(rng, 6), axis_at), (blocks,), jnp.float32, low / len(cuts), largest / len(cuts))
        factor_of = factor_of * jnp.repeat(jnp.exp(heights), extent[axis_at] // blocks).reshape((-1,) + (1,) * (len(extent) - 1 - axis_at))
    return factor_of


def centred(key, extent, width, limit, cuts=(), held_as=jnp.bfloat16):
    array = jax.random.normal(key, extent, jnp.float32) * width
    if len(cuts) > 0:
        array = block_scale(key, extent, cuts, -0.22, 0.18) * array
    return jnp.clip(array, min=-limit, max=limit).astype(held_as)


def setup_inputs(seed: int = 0) -> dict:
    keys = jax.random.split(jax.random.key(seed), 8)
    return {
        "concentration": draw_concentration(jax.random.fold_in(keys[7], 71), 0),
        "tissue_mask": draw_tissue_mask(jax.random.fold_in(keys[7], 71), 0),
        "wall_layer": draw_wall_layer(jax.random.fold_in(keys[7], 71), 0),
        "stiffness": jnp.clip(jnp.exp(math.log(2.0) - 0.6931472 * jax.random.uniform(keys[3], (NZ, NX, NY), jnp.float32) ** block_scale(keys[3], (NZ, NX, NY), ((0, 8), (1, 4)), -0.2, 0.2)), 1.0, 2.0),
        "production": centred(keys[4], (NZ, NX, NY), 0.5, 3.0, ((0, 8), (1, 4)), jnp.float32),
        "layer_diffusivity": jnp.clip(jnp.exp(jax.random.uniform(keys[5], (LAYERS,), jnp.float32, math.log(1.0), math.log(2.0))), 1.0, 2.0),
        "uptake_rate": jnp.clip(jnp.exp(jax.random.uniform(keys[6], (LAYERS,), jnp.float32, math.log(0.1), math.log(0.5))), 0.1, 0.5),
    }


SECTION_RATE = 0.05

def table_lookup(labels, coeffs):
    summed = jnp.zeros(labels.shape, jnp.float32)
    for layer_index in range(coeffs.shape[0]):
        summed = summed + jnp.where(labels == layer_index, coeffs[layer_index], 0.0)
    return summed

def lower_neighbour(values, axis_id):
    zero_plane = jnp.zeros_like(lax.slice_in_dim(values, 0, 1, axis=axis_id))
    kept = lax.slice_in_dim(values, 0, values.shape[axis_id] - 1, axis=axis_id)
    return jnp.concatenate([zero_plane, kept], axis=axis_id)

def upper_neighbour(values, axis_id):
    zero_plane = jnp.zeros_like(lax.slice_in_dim(values, 0, 1, axis=axis_id))
    kept = lax.slice_in_dim(values, 1, values.shape[axis_id], axis=axis_id)
    return jnp.concatenate([kept, zero_plane], axis=axis_id)

def axial_solve(lower_band, diagonal, upper_band, rhs_vals):

    def forward(carried, row_data):
        prev_ratio, prev_value = carried
        low_coef, diag_coef, high_coef, right_side = row_data
        pivot = diag_coef - low_coef * prev_ratio
        new_ratio = high_coef / pivot
        new_value = (right_side - low_coef * prev_value) / pivot
        return ((new_ratio, new_value), (new_ratio, new_value))
    zero_plane = jnp.zeros(rhs_vals.shape[1:], jnp.float32)
    _, (ratios, values) = lax.scan(forward, (zero_plane, zero_plane), (lower_band, diagonal, upper_band, rhs_vals))

    def backward(next_value, row_data):
        ratio_row, value_row = row_data
        solved_row = value_row - ratio_row * next_value
        return (solved_row, solved_row)
    _, solved = lax.scan(backward, zero_plane, (ratios, values), reverse=True)
    return solved

def reference(concentration, tissue_mask, wall_layer, stiffness, production, layer_diffusivity, uptake_rate):
    tissue_weight = tissue_mask.astype(jnp.float32)
    diffusivity = tissue_weight * table_lookup(wall_layer, layer_diffusivity) * stiffness
    uptake_cell = tissue_weight * table_lookup(wall_layer, uptake_rate)
    source_cell = tissue_weight * production
    weights = []
    for axis_id in range(3):
        weights.append((jnp.sqrt(diffusivity * lower_neighbour(diffusivity, axis_id)), jnp.sqrt(diffusivity * upper_neighbour(diffusivity, axis_id))))
    lower_band = -RZ * weights[0][0]
    upper_band = -RZ * weights[0][1]
    diagonal = 1.0 + RZ * (weights[0][0] + weights[0][1])
    state_now = concentration
    for step_index in range(STEPS):
        net_flux = jnp.zeros_like(state_now)
        for axis_id in (1, 2):
            net_flux = net_flux + weights[axis_id][0] * (lower_neighbour(state_now, axis_id) - state_now)
            net_flux = net_flux + weights[axis_id][1] * (upper_neighbour(state_now, axis_id) - state_now)
        explicit = state_now + SECTION_RATE * net_flux
        solved = axial_solve(lower_band, diagonal, upper_band, explicit)
        state_now = solved + (source_cell - uptake_cell * solved)
    return state_now
```

```python
import functools

import jax
import jax.numpy as jnp
from jax import lax
from jax.experimental import pallas as pl
from jax.experimental.pallas import tpu as pltpu
from jax.sharding import PartitionSpec as P

STEPS = 2
RZ = 3072
SECTION_RATE = 0.05
MESH = pl.DeviceIdType.MESH


def lookup(labels, table_ref):
    summed = jnp.zeros(labels.shape, jnp.float32)
    for index in range(table_ref.shape[0]):
        summed = jnp.where(labels == index, table_ref[index], summed)
    return summed


def kernel(
    n_ax, n_xs, chunk,
    conc_hbm, mask_hbm, layer_hbm, stiff_hbm, prod_hbm, diff_tab, upt_tab,
    out_ref,
    mask, layer, stiff, source, state, root, ratio, recip, prodr, part, plane, side, uptake,
    edge, halo, fixed, shut, outer_in, inner_in, a_send, b_send, rows,
    in_sem, xs_send, xs_recv, ax_send, ax_recv, a_ssem, a_rsem, b_ssem, b_rsem,
):
    m, slab, cols = conc_hbm.shape
    chunks = slab // chunk
    me = lax.axis_index("ax")
    mx = lax.axis_index("xs")
    half = n_ax // 2
    lower = me < half
    inner = jnp.where(lower, me + 1, me - 1)
    outer = jnp.where(lower, me - 1, me + 1)
    middle = (me == half - 1) | (me == half)
    has_outer = (me > 0) & (me < n_ax - 1)

    loads = [
        pltpu.make_async_copy(src, dst, in_sem.at[at])
        for at, (src, dst) in enumerate(
            [(mask_hbm, mask), (layer_hbm, layer), (stiff_hbm, stiff), (conc_hbm, state), (prod_hbm, source)]
        )
    ]
    for load in loads:
        load.start()

    sides = (
        (mx > 0, {"xs": mx - 1}),
        (mx < n_xs - 1, {"xs": mx + 1}),
        (me > 0, {"ax": me - 1}),
        (me < n_ax - 1, {"ax": me + 1}),
    )
    barrier = pltpu.get_barrier_semaphore()
    for there, peer in sides:
        @pl.when(there)
        def _(peer=peer):
            pl.semaphore_signal(barrier, inc=1, device_id=peer, device_id_type=MESH)

    for at in range(2):
        @pl.when(jnp.logical_not(sides[at][0]))
        def _(at=at):
            for slot in range(STEPS + 1):
                halo[slot, at] = jnp.zeros((m, 1, cols), jnp.float32)

    @pl.when(jnp.logical_not(sides[2][0]))
    def _():
        root[0] = jnp.zeros((slab, cols), jnp.float32)

    @pl.when(jnp.logical_not(sides[3][0]))
    def _():
        root[m + 1] = jnp.zeros((slab, cols), jnp.float32)

    @pl.when(jnp.logical_not(has_outer))
    def _():
        for step in range(STEPS):
            for at in range(2):
                outer_in[step, at] = jnp.zeros((slab, cols), jnp.float32)

    def xs_copy(slot, at):
        return pltpu.make_async_remote_copy(
            src_ref=edge.at[slot, at], dst_ref=halo.at[slot, 1 - at],
            send_sem=xs_send.at[slot, at], recv_sem=xs_recv.at[slot, 1 - at],
            device_id=sides[at][1], device_id_type=MESH,
        )

    def xs_start(slot):
        for at in range(2):
            @pl.when(sides[at][0])
            def _(at=at):
                xs_copy(slot, at).start()

    def xs_wait(slot):
        for at in range(2):
            @pl.when(sides[at][0])
            def _(at=at):
                xs_copy(slot, 1 - at).wait_recv()
                xs_copy(slot, at).wait_send()

    def ax_copy(at):
        src, dst = ((1, m + 1), (m, 0))[at]
        return pltpu.make_async_remote_copy(
            src_ref=root.at[src], dst_ref=root.at[dst],
            send_sem=ax_send.at[at], recv_sem=ax_recv.at[1 - at],
            device_id=sides[2 + at][1], device_id_type=MESH,
        )

    def set_root(z):
        diffusivity = mask[z].astype(jnp.float32) * lookup(layer[z], diff_tab) * stiff[z]
        value = jnp.sqrt(diffusivity)
        root[z + 1] = value
        edge[STEPS, 0, z] = value[0:1]
        edge[STEPS, 1, z] = value[slab - 1:slab]

    for load in loads[:3]:
        load.wait()
    set_root(0)
    set_root(m - 1)
    pl.semaphore_wait(barrier, sum(jnp.where(there, 1, 0) for there, _ in sides))
    for at in range(2):
        @pl.when(sides[2 + at][0])
        def _(at=at):
            ax_copy(at).start()

    loads[3].wait()

    def copy_edges(z, carry):
        edge[0, 0, z] = state[z, 0:1]
        edge[0, 1, z] = state[z, slab - 1:slab]
        return carry

    lax.fori_loop(0, m, copy_edges, 0)
    xs_start(0)

    def root_body(z, carry):
        set_root(z)
        return carry

    lax.fori_loop(1, m - 1, root_body, 0)
    xs_start(STEPS)
    loads[4].wait()

    def cell_body(z, carry):
        weight = mask[z].astype(jnp.float32)
        uptake[z] = weight * lookup(layer[z], upt_tab)
        source[z] = weight * source[z]
        return carry

    lax.fori_loop(0, m, cell_body, 0)
    for at in range(2):
        @pl.when(sides[2 + at][0])
        def _(at=at):
            ax_copy(1 - at).wait_recv()
            ax_copy(at).wait_send()

    band_first = RZ * root[0] * root[1]
    rows[0] = band_first

    def factor_body(z, carry):
        excess, product, total = carry
        band = (RZ * root[z + 1]) * root[z + 2]
        inverse = 1.0 / (excess + band)
        ratio_now = band * inverse
        scaled = product * inverse
        ratio[z] = ratio_now
        recip[z] = inverse
        prodr[z] = scaled
        return 1.0 + ratio_now * excess, product * ratio_now, total + product * scaled

    ones = jnp.ones((slab, cols), jnp.float32)
    _, through_up, total = lax.fori_loop(0, m, factor_body, (1.0 + band_first, ones, 0.0 * ones))
    alpha_low = band_first * total
    alpha_high = through_up
    beta_low = band_first * prodr[m - 1]
    beta_high = ratio[m - 1]
    fixed[0] = jnp.where(lower, alpha_low, beta_high)
    fixed[1] = jnp.where(lower, alpha_high, beta_low)
    fixed[2] = jnp.where(lower, beta_low, alpha_high)
    fixed[3] = jnp.where(lower, beta_high, alpha_low)

    xs_wait(STEPS)
    row_at = lax.broadcasted_iota(jnp.int32, (slab, cols), 0)
    col_at = lax.broadcasted_iota(jnp.int32, (slab, cols), 1)

    def plane_body(z, carry):
        value = root[z + 1]
        scaled = SECTION_RATE * value
        above = jnp.where(row_at == 0, halo[STEPS, 0, z], pltpu.roll(value, 1, 0))
        plane[z] = scaled * above
        shut[z] = scaled[slab - 1:slab] * halo[STEPS, 1, z]
        side[z] = jnp.where(col_at == 0, 0.0, scaled * pltpu.roll(value, 1, 1))
        return carry

    lax.fori_loop(0, m, plane_body, 0)

    def a_copy(step, c, to_middle):
        cut = pl.ds(c * chunk, chunk)
        pick = pl.ds(0, 2 if step == 0 else 1)
        return pltpu.make_async_remote_copy(
            src_ref=a_send.at[step, pick, cut],
            dst_ref=(inner_in if to_middle else outer_in).at[step, pick, cut],
            send_sem=a_ssem.at[step, c],
            recv_sem=(b_rsem if to_middle else a_rsem).at[step, c],
            device_id={"ax": inner}, device_id_type=MESH,
        )

    def b_copy(step, c):
        cut = pl.ds(c * chunk, chunk)
        return pltpu.make_async_remote_copy(
            src_ref=b_send.at[step, 0, cut], dst_ref=inner_in.at[step, 0, cut],
            send_sem=b_ssem.at[step, c], recv_sem=b_rsem.at[step, c],
            device_id={"ax": outer}, device_id_type=MESH,
        )

    for step in range(STEPS):
        xs_wait(step)

        def forward_body(z, carry):
            moved, first = carry
            now = state[z]
            above = jnp.where(row_at == 0, halo[step, 0, z], pltpu.roll(now, 1, 0))
            flux = plane[z] * (above - now)
            closing = shut[z] * (now[slab - 1:slab] - halo[step, 1, z])
            below = jnp.where(row_at == slab - 1, closing, pltpu.roll(flux, slab - 1, 0))
            across = side[z] * (pltpu.roll(now, 1, 1) - now)
            explicit = now + ((flux - below) + (across - pltpu.roll(across, cols - 1, 1)))
            value = explicit + moved
            part[z] = recip[z] * value
            return ratio[z] * value, first + prodr[z] * value

        _, first = lax.fori_loop(0, m, forward_body, (0.0 * ones, 0.0 * ones))
        last = part[m - 1]
        rows[1] = jnp.where(lower, first, last)
        rows[2] = jnp.where(lower, last, first)

        for c in range(chunks):
            cut = slice(c * chunk, (c + 1) * chunk)

            @pl.when(has_outer)
            def _(step=step, c=c):
                a_copy(step, c, False).wait_recv()

            link = outer_in[0, 1, cut]
            if step == 0:
                gain = 1.0 / (1.0 - link * fixed[0, cut])
                fixed[4, cut] = gain
                a_send[0, 1, cut] = fixed[3, cut] + fixed[2, cut] * (gain * link * fixed[1, cut])
                fixed[5, cut] = gain * link * fixed[1, cut]
            known = fixed[4, cut] * (outer_in[step, 0, cut] + link * rows[1, cut])
            rows[3, cut] = known
            a_send[step, 0, cut] = rows[2, cut] + fixed[2, cut] * known

            @pl.when(middle)
            def _(step=step, c=c):
                a_copy(step, c, True).start()

            @pl.when(jnp.logical_not(middle))
            def _(step=step, c=c):
                a_copy(step, c, False).start()

        for c in range(chunks):
            cut = slice(c * chunk, (c + 1) * chunk)

            @pl.when(middle)
            def _(step=step, c=c, cut=cut):
                a_copy(step, c, True).wait_recv()
                own, own_link = a_send[step, 0, cut], a_send[0, 1, cut]
                far, far_link = inner_in[step, 0, cut], inner_in[0, 1, cut]
                if step == 0:
                    fixed[6, cut] = 1.0 / (1.0 - own_link * far_link)
                rows[4, cut] = far + far_link * ((own + own_link * far) * fixed[6, cut])

            @pl.when(jnp.logical_not(middle))
            def _(step=step, c=c, cut=cut):
                b_copy(step, c).wait_recv()
                rows[4, cut] = inner_in[step, 0, cut]

            inner_value = rows[4, cut]
            outer_value = rows[3, cut] + fixed[5, cut] * inner_value
            rows[5, cut] = outer_value
            b_send[step, 0, cut] = rows[1, cut] + fixed[0, cut] * outer_value + fixed[1, cut] * inner_value

            @pl.when(has_outer)
            def _(step=step, c=c):
                b_copy(step, c).start()

        below_value = rows[0] * jnp.where(lower, rows[5], rows[4])
        above_value = jnp.where(lower, rows[4], rows[5])
        final = step == STEPS - 1

        def backward_body(at, later):
            z = m - 1 - at
            solved = part[z] + prodr[z] * below_value + ratio[z] * later
            after = solved + (source[z] - uptake[z] * solved)
            if final:
                out_ref[z] = after
            else:
                state[z] = after
                edge[step + 1, 0, z] = after[0:1]
                edge[step + 1, 1, z] = after[slab - 1:slab]
            return solved

        lax.fori_loop(0, m, backward_body, above_value)
        if not final:
            xs_start(step + 1)

    for step in range(STEPS):
        for c in range(chunks):
            a_copy(step, c, False).wait_send()

            @pl.when(has_outer)
            def _(step=step, c=c):
                b_copy(step, c).wait_send()


def on_device(n_ax, n_xs, conc, mask, layer, stiff, prod, diff_tab, upt_tab):
    m, slab, cols = conc.shape
    chunk = 8 if slab % 8 == 0 else slab
    chunks = slab // chunk
    f32 = jnp.float32
    cells = pltpu.VMEM((m, slab, cols), f32)
    labels = pltpu.VMEM((m, slab, cols), jnp.int32)
    dma = pltpu.SemaphoreType.DMA
    vmem = lambda *shape: pltpu.VMEM(shape, f32)
    any_spec = pl.BlockSpec(memory_space=pl.ANY)
    smem_spec = pl.BlockSpec(memory_space=pltpu.SMEM)
    return pl.pallas_call(
        functools.partial(kernel, n_ax, n_xs, chunk),
        out_shape=jax.ShapeDtypeStruct((m, slab, cols), f32),
        in_specs=[any_spec] * 5 + [smem_spec] * 2,
        out_specs=pl.BlockSpec(memory_space=pltpu.VMEM),
        scratch_shapes=[
            labels, labels, cells, cells, cells, vmem(m + 2, slab, cols),
            cells, cells, cells, cells, cells, cells, cells,
            vmem(STEPS + 1, 2, m, 1, cols), vmem(STEPS + 1, 2, m, 1, cols),
            vmem(7, slab, cols), vmem(m, 1, cols),
            vmem(STEPS, 2, slab, cols), vmem(STEPS, 2, slab, cols),
            vmem(STEPS, 2, slab, cols), vmem(STEPS, 1, slab, cols), vmem(6, slab, cols),
            dma((5,)), dma((STEPS + 1, 2)), dma((STEPS + 1, 2)), dma((2,)), dma((2,)),
            dma((STEPS, chunks)), dma((STEPS, chunks)), dma((STEPS, chunks)), dma((STEPS, chunks)),
        ],
        compiler_params=pltpu.CompilerParams(
            collective_id=0, has_side_effects=True, vmem_limit_bytes=56 * 1024 * 1024
        ),
    )(conc, mask, layer, stiff, prod, diff_tab, upt_tab)


def solution(mesh):
    cells = P("ax", "xs", None)
    return jax.shard_map(
        functools.partial(on_device, mesh.shape["ax"], mesh.shape["xs"]),
        mesh=mesh, in_specs=(cells,) * 5 + (P(), P()), out_specs=cells, check_vma=False,
    )
```

```python
import functools

import jax
import jax.numpy as jnp
from jax import lax
from jax.experimental import pallas as pl
from jax.experimental.pallas import tpu as pltpu
from jax.sharding import PartitionSpec as P

STEPS = 2
RZ = 3072
SECTION_RATE = 0.05
MESH = pl.DeviceIdType.MESH


def lookup(labels, table_ref):
    summed = jnp.zeros(labels.shape, jnp.float32)
    for index in range(table_ref.shape[0]):
        summed = jnp.where(labels == index, table_ref[index], summed)
    return summed


def kernel(
    n_ax, n_xs, chunk,
    conc_hbm, mask_hbm, layer_hbm, stiff_hbm, prod_hbm, diff_tab, upt_tab,
    out_ref,
    mask, layer, stiff, source, state, root, ratio, recip, prodr, part, plane, side, uptake,
    edge, halo, fixed, shut, outer_in, inner_in, a_send, b_send, rows,
    in_sem, xs_send, xs_recv, ax_send, ax_recv, a_ssem, a_rsem, b_ssem, b_rsem,
):
    m, slab, cols = conc_hbm.shape
    chunks = slab // chunk
    me = lax.axis_index("ax")
    mx = lax.axis_index("xs")
    half = n_ax // 2
    lower = me < half
    inner = jnp.where(lower, me + 1, me - 1)
    outer = jnp.where(lower, me - 1, me + 1)
    middle = (me == half - 1) | (me == half)
    has_outer = (me > 0) & (me < n_ax - 1)

    loads = [
        pltpu.make_async_copy(src, dst, in_sem.at[at])
        for at, (src, dst) in enumerate(
            [(mask_hbm, mask), (layer_hbm, layer), (stiff_hbm, stiff), (conc_hbm, state), (prod_hbm, source)]
        )
    ]
    for load in loads:
        load.start()

    sides = (
        (mx > 0, {"xs": mx - 1}),
        (mx < n_xs - 1, {"xs": mx + 1}),
        (me > 0, {"ax": me - 1}),
        (me < n_ax - 1, {"ax": me + 1}),
    )
    barrier = pltpu.get_barrier_semaphore()
    for there, peer in sides:
        @pl.when(there)
        def _(peer=peer):
            pl.semaphore_signal(barrier, inc=1, device_id=peer, device_id_type=MESH)

    for at in range(2):
        @pl.when(jnp.logical_not(sides[at][0]))
        def _(at=at):
            for slot in range(STEPS + 1):
                halo[slot, at] = jnp.zeros((m, 1, cols), jnp.float32)

    @pl.when(jnp.logical_not(sides[2][0]))
    def _():
        root[0] = jnp.zeros((slab, cols), jnp.float32)

    @pl.when(jnp.logical_not(sides[3][0]))
    def _():
        root[m + 1] = jnp.zeros((slab, cols), jnp.float32)

    @pl.when(jnp.logical_not(has_outer))
    def _():
        for step in range(STEPS):
            for at in range(2):
                outer_in[step, at] = jnp.zeros((slab, cols), jnp.float32)

    def xs_copy(slot, at):
        return pltpu.make_async_remote_copy(
            src_ref=edge.at[slot, at], dst_ref=halo.at[slot, 1 - at],
            send_sem=xs_send.at[slot, at], recv_sem=xs_recv.at[slot, 1 - at],
            device_id=sides[at][1], device_id_type=MESH,
        )

    def xs_start(slot):
        for at in range(2):
            @pl.when(sides[at][0])
            def _(at=at):
                xs_copy(slot, at).start()

    def xs_wait(slot):
        for at in range(2):
            @pl.when(sides[at][0])
            def _(at=at):
                xs_copy(slot, 1 - at).wait_recv()
                xs_copy(slot, at).wait_send()

    def ax_copy(at):
        src, dst = ((1, m + 1), (m, 0))[at]
        return pltpu.make_async_remote_copy(
            src_ref=root.at[src], dst_ref=root.at[dst],
            send_sem=ax_send.at[at], recv_sem=ax_recv.at[1 - at],
            device_id=sides[2 + at][1], device_id_type=MESH,
        )

    def set_root(z):
        diffusivity = mask[z].astype(jnp.float32) * lookup(layer[z], diff_tab) * stiff[z]
        value = jnp.sqrt(diffusivity)
        root[z + 1] = value
        edge[STEPS, 0, z] = value[0:1]
        edge[STEPS, 1, z] = value[slab - 1:slab]

    for load in loads[:3]:
        load.wait()
    set_root(0)
    set_root(m - 1)
    pl.semaphore_wait(barrier, sum(jnp.where(there, 1, 0) for there, _ in sides))
    for at in range(2):
        @pl.when(sides[2 + at][0])
        def _(at=at):
            ax_copy(at).start()

    loads[3].wait()

    def copy_edges(z, carry):
        edge[0, 0, z] = state[z, 0:1]
        edge[0, 1, z] = state[z, slab - 1:slab]
        return carry

    lax.fori_loop(0, m, copy_edges, 0)
    xs_start(0)

    def root_body(z, carry):
        set_root(z)
        return carry

    lax.fori_loop(1, m - 1, root_body, 0, unroll=2)
    xs_start(STEPS)
    for at in range(2):
        @pl.when(sides[2 + at][0])
        def _(at=at):
            ax_copy(1 - at).wait_recv()
            ax_copy(at).wait_send()

    band_first = RZ * root[0] * root[1]
    rows[0] = band_first

    def factor_body(z, carry):
        excess, product, total = carry
        band = (RZ * root[z + 1]) * root[z + 2]
        inverse = 1.0 / (excess + band)
        ratio_now = band * inverse
        scaled = product * inverse
        ratio[z] = ratio_now
        recip[z] = inverse
        prodr[z] = scaled
        return 1.0 + ratio_now * excess, product * ratio_now, total + product * scaled

    ones = jnp.ones((slab, cols), jnp.float32)
    _, through_up, total = lax.fori_loop(0, m, factor_body, (1.0 + band_first, ones, 0.0 * ones), unroll=2)
    alpha_low = band_first * total
    alpha_high = through_up
    beta_low = band_first * prodr[m - 1]
    beta_high = ratio[m - 1]
    fixed[0] = jnp.where(lower, alpha_low, beta_high)
    fixed[1] = jnp.where(lower, alpha_high, beta_low)
    fixed[2] = jnp.where(lower, beta_low, alpha_high)
    fixed[3] = jnp.where(lower, beta_high, alpha_low)

    xs_wait(STEPS)
    row_at = lax.broadcasted_iota(jnp.int32, (slab, cols), 0)
    col_at = lax.broadcasted_iota(jnp.int32, (slab, cols), 1)

    def plane_body(z, carry):
        value = root[z + 1]
        scaled = SECTION_RATE * value
        above = jnp.where(row_at == 0, halo[STEPS, 0, z], pltpu.roll(value, 1, 0))
        plane[z] = scaled * above
        shut[z] = scaled[slab - 1:slab] * halo[STEPS, 1, z]
        side[z] = jnp.where(col_at == 0, 0.0, scaled * pltpu.roll(value, 1, 1))
        return carry

    lax.fori_loop(0, m, plane_body, 0, unroll=2)

    def a_copy(step, c, to_middle):
        cut = pl.ds(c * chunk, chunk)
        pick = pl.ds(0, 2 if step == 0 else 1)
        return pltpu.make_async_remote_copy(
            src_ref=a_send.at[step, pick, cut],
            dst_ref=(inner_in if to_middle else outer_in).at[step, pick, cut],
            send_sem=a_ssem.at[step, c],
            recv_sem=(b_rsem if to_middle else a_rsem).at[step, c],
            device_id={"ax": inner}, device_id_type=MESH,
        )

    def b_copy(step, c):
        cut = pl.ds(c * chunk, chunk)
        return pltpu.make_async_remote_copy(
            src_ref=b_send.at[step, 0, cut], dst_ref=inner_in.at[step, 0, cut],
            send_sem=b_ssem.at[step, c], recv_sem=b_rsem.at[step, c],
            device_id={"ax": outer}, device_id_type=MESH,
        )

    loads[4].wait()

    def cell_body(z, carry):
        weight = mask[z].astype(jnp.float32)
        uptake[z] = weight * lookup(layer[z], upt_tab)
        source[z] = weight * source[z]
        return carry

    def cell_loop():
        lax.fori_loop(0, m, cell_body, 0, unroll=2)

    if chunks > 2:
        inside = ((chunk, slab - chunk),)
        ends = ((0, chunk), (slab - chunk, slab))
        order = tuple(range(1, chunks - 1)) + (0, chunks - 1)
    else:
        inside, ends, order = (), ((0, slab),), tuple(range(chunks))
    early = order[:chunks - 2] if inside else ()

    for step in range(STEPS):

        def forward(ranges):
            def body(z, carries):
                done = []
                for (lo, hi), (moved, first) in zip(ranges, carries):
                    span = slice(lo, hi)
                    size = hi - lo
                    row = lax.broadcasted_iota(jnp.int32, (size, cols), 0)
                    now = state[z, span]
                    before = halo[step, 0, z] if lo == 0 else state[z, lo - 1:lo]
                    above = jnp.where(row == 0, before, pltpu.roll(now, 1, 0))
                    flux = plane[z, span] * (above - now)
                    if hi == slab:
                        closing = shut[z] * (now[size - 1:size] - halo[step, 1, z])
                    else:
                        closing = plane[z, hi:hi + 1] * (now[size - 1:size] - state[z, hi:hi + 1])
                    below = jnp.where(row == size - 1, closing, pltpu.roll(flux, size - 1, 0))
                    across = side[z, span] * (pltpu.roll(now, 1, 1) - now)
                    explicit = now + ((flux - below) + (across - pltpu.roll(across, cols - 1, 1)))
                    value = explicit + moved
                    part[z, span] = recip[z, span] * value
                    done.append((ratio[z, span] * value, first + prodr[z, span] * value))
                return tuple(done)

            zeros = [jnp.zeros((hi - lo, cols), jnp.float32) for lo, hi in ranges]
            sums = lax.fori_loop(0, m, body, tuple((zero, zero) for zero in zeros), unroll=2)
            for (lo, hi), (_, first) in zip(ranges, sums):
                span = slice(lo, hi)
                last = part[m - 1, span]
                rows[1, span] = jnp.where(lower, first, last)
                rows[2, span] = jnp.where(lower, last, first)

        def inward(c):
            cut = slice(c * chunk, (c + 1) * chunk)

            @pl.when(has_outer)
            def _(step=step, c=c):
                a_copy(step, c, False).wait_recv()

            link = outer_in[0, 1, cut]
            if step == 0:
                gain = 1.0 / (1.0 - link * fixed[0, cut])
                fixed[4, cut] = gain
                a_send[0, 1, cut] = fixed[3, cut] + fixed[2, cut] * (gain * link * fixed[1, cut])
                fixed[5, cut] = gain * link * fixed[1, cut]
            known = fixed[4, cut] * (outer_in[step, 0, cut] + link * rows[1, cut])
            rows[3, cut] = known
            a_send[step, 0, cut] = rows[2, cut] + fixed[2, cut] * known

            @pl.when(middle)
            def _(step=step, c=c):
                a_copy(step, c, True).start()

            @pl.when(jnp.logical_not(middle))
            def _(step=step, c=c):
                a_copy(step, c, False).start()

        if inside:
            forward(inside)

            @pl.when(jnp.logical_not(has_outer))
            def _():
                for c in early:
                    inward(c)

        xs_wait(step)
        forward(ends)
        if step == 0:
            pl.when(has_outer)(cell_loop)

        @pl.when(has_outer)
        def _():
            for c in order:
                inward(c)

        @pl.when(jnp.logical_not(has_outer))
        def _():
            for c in order[len(early):]:
                inward(c)
            if step == 0:
                cell_loop()

        for c in order:
            cut = slice(c * chunk, (c + 1) * chunk)

            @pl.when(middle)
            def _(step=step, c=c, cut=cut):
                a_copy(step, c, True).wait_recv()
                own, own_link = a_send[step, 0, cut], a_send[0, 1, cut]
                far, far_link = inner_in[step, 0, cut], inner_in[0, 1, cut]
                if step == 0:
                    fixed[6, cut] = 1.0 / (1.0 - own_link * far_link)
                rows[4, cut] = far + far_link * ((own + own_link * far) * fixed[6, cut])

            @pl.when(jnp.logical_not(middle))
            def _(step=step, c=c, cut=cut):
                b_copy(step, c).wait_recv()
                rows[4, cut] = inner_in[step, 0, cut]

            inner_value = rows[4, cut]
            outer_value = rows[3, cut] + fixed[5, cut] * inner_value
            rows[5, cut] = outer_value
            b_send[step, 0, cut] = rows[1, cut] + fixed[0, cut] * outer_value + fixed[1, cut] * inner_value

            @pl.when(has_outer)
            def _(step=step, c=c):
                b_copy(step, c).start()

        final = step == STEPS - 1

        def backward(ranges):
            lows = []
            highs = []
            for lo, hi in ranges:
                span = slice(lo, hi)
                lows.append(rows[0, span] * jnp.where(lower, rows[5, span], rows[4, span]))
                highs.append(jnp.where(lower, rows[4, span], rows[5, span]))

            def body(at, carries):
                z = m - 1 - at
                done = []
                for (lo, hi), low, later in zip(ranges, lows, carries):
                    span = slice(lo, hi)
                    solved = part[z, span] + prodr[z, span] * low + ratio[z, span] * later
                    after = solved + (source[z, span] - uptake[z, span] * solved)
                    if final:
                        out_ref[z, span] = after
                    else:
                        state[z, span] = after
                        if lo == 0:
                            edge[step + 1, 0, z] = after[0:1]
                        if hi == slab:
                            edge[step + 1, 1, z] = after[hi - lo - 1:hi - lo]
                    done.append(solved)
                return tuple(done)

            lax.fori_loop(0, m, body, tuple(highs), unroll=2)

        if final:
            backward(((0, slab),))
        else:
            backward(ends)
            xs_start(step + 1)
            if inside:
                backward(inside)

    for step in range(STEPS):
        for c in range(chunks):
            a_copy(step, c, False).wait_send()

            @pl.when(has_outer)
            def _(step=step, c=c):
                b_copy(step, c).wait_send()


def on_device(n_ax, n_xs, conc, mask, layer, stiff, prod, diff_tab, upt_tab):
    m, slab, cols = conc.shape
    chunk = 8 if slab % 8 == 0 else slab
    chunks = slab // chunk
    f32 = jnp.float32
    cells = pltpu.VMEM((m, slab, cols), f32)
    labels = pltpu.VMEM((m, slab, cols), jnp.int32)
    dma = pltpu.SemaphoreType.DMA
    vmem = lambda *shape: pltpu.VMEM(shape, f32)
    any_spec = pl.BlockSpec(memory_space=pl.ANY)
    smem_spec = pl.BlockSpec(memory_space=pltpu.SMEM)
    return pl.pallas_call(
        functools.partial(kernel, n_ax, n_xs, chunk),
        out_shape=jax.ShapeDtypeStruct((m, slab, cols), f32),
        in_specs=[any_spec] * 5 + [smem_spec] * 2,
        out_specs=pl.BlockSpec(memory_space=pltpu.VMEM),
        scratch_shapes=[
            labels, labels, cells, cells, cells, vmem(m + 2, slab, cols),
            cells, cells, cells, cells, cells, cells, cells,
            vmem(STEPS + 1, 2, m, 1, cols), vmem(STEPS + 1, 2, m, 1, cols),
            vmem(7, slab, cols), vmem(m, 1, cols),
            vmem(STEPS, 2, slab, cols), vmem(STEPS, 2, slab, cols),
            vmem(STEPS, 2, slab, cols), vmem(STEPS, 1, slab, cols), vmem(6, slab, cols),
            dma((5,)), dma((STEPS + 1, 2)), dma((STEPS + 1, 2)), dma((2,)), dma((2,)),
            dma((STEPS, chunks)), dma((STEPS, chunks)), dma((STEPS, chunks)), dma((STEPS, chunks)),
        ],
        compiler_params=pltpu.CompilerParams(
            collective_id=0, has_side_effects=True, vmem_limit_bytes=56 * 1024 * 1024
        ),
    )(conc, mask, layer, stiff, prod, diff_tab, upt_tab)


def solution(mesh):
    cells = P("ax", "xs", None)
    return jax.shard_map(
        functools.partial(on_device, mesh.shape["ax"], mesh.shape["xs"]),
        mesh=mesh, in_specs=(cells,) * 5 + (P(), P()), out_specs=cells, check_vma=False,
    )
```

```python
import functools

import jax
import jax.numpy as jnp
from jax import lax
from jax.experimental import pallas as pl
from jax.experimental.pallas import tpu as pltpu
from jax.sharding import PartitionSpec as P

STEPS = 2
RZ = 3072
SECTION_RATE = 0.05
MESH = pl.DeviceIdType.MESH


def lookup(labels, table_ref):
    summed = jnp.zeros(labels.shape, jnp.float32)
    for index in range(table_ref.shape[0]):
        summed = jnp.where(labels == index, table_ref[index], summed)
    return summed


def kernel(
    n_ax, n_xs, chunk,
    conc_hbm, mask_hbm, layer_hbm, stiff_hbm, prod_hbm, diff_tab, upt_tab,
    out_ref,
    mask, layer, stiff, source, state, root, ratio, recip, prodr, part, plane, side, uptake,
    edge, halo, fixed, shut, outer_in, inner_in, a_send, b_send, rows,
    in_sem, xs_send, xs_recv, ax_send, ax_recv, a_ssem, a_rsem, b_ssem, b_rsem,
):
    m, slab, cols = conc_hbm.shape
    chunks = slab // chunk
    me = lax.axis_index("ax")
    mx = lax.axis_index("xs")
    half = n_ax // 2
    lower = me < half
    inner = jnp.where(lower, me + 1, me - 1)
    outer = jnp.where(lower, me - 1, me + 1)
    middle = (me == half - 1) | (me == half)
    has_outer = (me > 0) & (me < n_ax - 1)

    loads = [
        pltpu.make_async_copy(src, dst, in_sem.at[at])
        for at, (src, dst) in enumerate(
            [(mask_hbm, mask), (layer_hbm, layer), (stiff_hbm, stiff), (conc_hbm, state), (prod_hbm, source)]
        )
    ]
    for load in loads:
        load.start()

    sides = (
        (mx > 0, {"xs": mx - 1}),
        (mx < n_xs - 1, {"xs": mx + 1}),
        (me > 0, {"ax": me - 1}),
        (me < n_ax - 1, {"ax": me + 1}),
    )
    barrier = pltpu.get_barrier_semaphore()
    for there, peer in sides:
        @pl.when(there)
        def _(peer=peer):
            pl.semaphore_signal(barrier, inc=1, device_id=peer, device_id_type=MESH)

    for at in range(2):
        @pl.when(jnp.logical_not(sides[at][0]))
        def _(at=at):
            for slot in range(STEPS + 1):
                halo[slot, at] = jnp.zeros((m, 1, cols), jnp.float32)

    @pl.when(jnp.logical_not(sides[2][0]))
    def _():
        root[0] = jnp.zeros((slab, cols), jnp.float32)

    @pl.when(jnp.logical_not(sides[3][0]))
    def _():
        root[m + 1] = jnp.zeros((slab, cols), jnp.float32)

    @pl.when(jnp.logical_not(has_outer))
    def _():
        for step in range(STEPS):
            for at in range(2):
                outer_in[step, at] = jnp.zeros((slab, cols), jnp.float32)

    def xs_copy(slot, at):
        return pltpu.make_async_remote_copy(
            src_ref=edge.at[slot, at], dst_ref=halo.at[slot, 1 - at],
            send_sem=xs_send.at[slot, at], recv_sem=xs_recv.at[slot, 1 - at],
            device_id=sides[at][1], device_id_type=MESH,
        )

    def xs_start(slot):
        for at in range(2):
            @pl.when(sides[at][0])
            def _(at=at):
                xs_copy(slot, at).start()

    def xs_wait(slot):
        for at in range(2):
            @pl.when(sides[at][0])
            def _(at=at):
                xs_copy(slot, 1 - at).wait_recv()
                xs_copy(slot, at).wait_send()

    def ax_copy(at):
        src, dst = ((1, m + 1), (m, 0))[at]
        return pltpu.make_async_remote_copy(
            src_ref=root.at[src], dst_ref=root.at[dst],
            send_sem=ax_send.at[at], recv_sem=ax_recv.at[1 - at],
            device_id=sides[2 + at][1], device_id_type=MESH,
        )

    def set_root(z):
        diffusivity = mask[z].astype(jnp.float32) * lookup(layer[z], diff_tab) * stiff[z]
        value = jnp.sqrt(diffusivity)
        root[z + 1] = value
        edge[STEPS, 0, z] = value[0:1]
        edge[STEPS, 1, z] = value[slab - 1:slab]

    for load in loads[:3]:
        load.wait()
    set_root(0)
    set_root(m - 1)
    pl.semaphore_wait(barrier, sum(jnp.where(there, 1, 0) for there, _ in sides))
    for at in range(2):
        @pl.when(sides[2 + at][0])
        def _(at=at):
            ax_copy(at).start()

    loads[3].wait()

    def copy_edges(z, carry):
        edge[0, 0, z] = state[z, 0:1]
        edge[0, 1, z] = state[z, slab - 1:slab]
        return carry

    lax.fori_loop(0, m, copy_edges, 0, unroll=8)
    xs_start(0)

    def root_body(z, carry):
        set_root(z)
        return carry

    lax.fori_loop(1, m - 1, root_body, 0, unroll=6)
    xs_start(STEPS)
    for at in range(2):
        @pl.when(sides[2 + at][0])
        def _(at=at):
            ax_copy(1 - at).wait_recv()
            ax_copy(at).wait_send()

    band_first = RZ * root[0] * root[1]
    rows[0] = band_first

    def factor_body(z, carry):
        excess, product, total = carry
        band = (RZ * root[z + 1]) * root[z + 2]
        inverse = 1.0 / (excess + band)
        ratio_now = band * inverse
        scaled = product * inverse
        ratio[z] = ratio_now
        recip[z] = inverse
        prodr[z] = scaled
        return 1.0 + ratio_now * excess, product * ratio_now, total + product * scaled

    ones = jnp.ones((slab, cols), jnp.float32)
    _, through_up, total = lax.fori_loop(0, m, factor_body, (1.0 + band_first, ones, 0.0 * ones), unroll=8)
    alpha_low = band_first * total
    alpha_high = through_up
    beta_low = band_first * prodr[m - 1]
    beta_high = ratio[m - 1]
    fixed[0] = jnp.where(lower, alpha_low, beta_high)
    fixed[1] = jnp.where(lower, alpha_high, beta_low)
    fixed[2] = jnp.where(lower, beta_low, alpha_high)
    fixed[3] = jnp.where(lower, beta_high, alpha_low)

    xs_wait(STEPS)
    row_at = lax.broadcasted_iota(jnp.int32, (slab, cols), 0)
    col_at = lax.broadcasted_iota(jnp.int32, (slab, cols), 1)

    def plane_body(z, carry):
        value = root[z + 1]
        scaled = SECTION_RATE * value
        above = jnp.where(row_at == 0, halo[STEPS, 0, z], pltpu.roll(value, 1, 0))
        plane[z] = scaled * above
        shut[z] = scaled[slab - 1:slab] * halo[STEPS, 1, z]
        side[z] = jnp.where(col_at == 0, 0.0, scaled * pltpu.roll(value, 1, 1))
        return carry

    lax.fori_loop(0, m, plane_body, 0, unroll=8)

    def a_copy(step, c, to_middle):
        cut = pl.ds(c * chunk, chunk)
        pick = pl.ds(0, 2 if step == 0 else 1)
        return pltpu.make_async_remote_copy(
            src_ref=a_send.at[step, pick, cut],
            dst_ref=(inner_in if to_middle else outer_in).at[step, pick, cut],
            send_sem=a_ssem.at[step, c],
            recv_sem=(b_rsem if to_middle else a_rsem).at[step, c],
            device_id={"ax": inner}, device_id_type=MESH,
        )

    def b_copy(step, c):
        cut = pl.ds(c * chunk, chunk)
        return pltpu.make_async_remote_copy(
            src_ref=b_send.at[step, 0, cut], dst_ref=inner_in.at[step, 0, cut],
            send_sem=b_ssem.at[step, c], recv_sem=b_rsem.at[step, c],
            device_id={"ax": outer}, device_id_type=MESH,
        )

    loads[4].wait()

    def cell_body(z, carry):
        weight = mask[z].astype(jnp.float32)
        uptake[z] = weight * lookup(layer[z], upt_tab)
        source[z] = weight * source[z]
        return carry

    def cell_loop():
        lax.fori_loop(0, m, cell_body, 0, unroll=8)

    if chunks > 2:
        inside = ((chunk, slab - chunk),)
        ends = ((0, chunk), (slab - chunk, slab))
        order = tuple(range(1, chunks - 1)) + (0, chunks - 1)
    else:
        inside, ends, order = (), ((0, slab),), tuple(range(chunks))
    early = order[:chunks - 2] if inside else ()

    for step in range(STEPS):

        def forward(ranges):
            def body(z, carries):
                done = []
                for (lo, hi), (moved, first) in zip(ranges, carries):
                    span = slice(lo, hi)
                    size = hi - lo
                    row = lax.broadcasted_iota(jnp.int32, (size, cols), 0)
                    now = state[z, span]
                    before = halo[step, 0, z] if lo == 0 else state[z, lo - 1:lo]
                    above = jnp.where(row == 0, before, pltpu.roll(now, 1, 0))
                    flux = plane[z, span] * (above - now)
                    if hi == slab:
                        closing = shut[z] * (now[size - 1:size] - halo[step, 1, z])
                    else:
                        closing = plane[z, hi:hi + 1] * (now[size - 1:size] - state[z, hi:hi + 1])
                    below = jnp.where(row == size - 1, closing, pltpu.roll(flux, size - 1, 0))
                    across = side[z, span] * (pltpu.roll(now, 1, 1) - now)
                    explicit = now + ((flux - below) + (across - pltpu.roll(across, cols - 1, 1)))
                    value = explicit + moved
                    part[z, span] = recip[z, span] * value
                    done.append((ratio[z, span] * value, first + prodr[z, span] * value))
                return tuple(done)

            zeros = [jnp.zeros((hi - lo, cols), jnp.float32) for lo, hi in ranges]
            sums = lax.fori_loop(0, m, body, tuple((zero, zero) for zero in zeros), unroll=8)
            for (lo, hi), (_, first) in zip(ranges, sums):
                span = slice(lo, hi)
                last = part[m - 1, span]
                rows[1, span] = jnp.where(lower, first, last)
                rows[2, span] = jnp.where(lower, last, first)

        def inward(c):
            cut = slice(c * chunk, (c + 1) * chunk)

            @pl.when(has_outer)
            def _(step=step, c=c):
                a_copy(step, c, False).wait_recv()

            link = outer_in[0, 1, cut]
            if step == 0:
                gain = 1.0 / (1.0 - link * fixed[0, cut])
                fixed[4, cut] = gain
                a_send[0, 1, cut] = fixed[3, cut] + fixed[2, cut] * (gain * link * fixed[1, cut])
                fixed[5, cut] = gain * link * fixed[1, cut]
            known = fixed[4, cut] * (outer_in[step, 0, cut] + link * rows[1, cut])
            rows[3, cut] = known
            a_send[step, 0, cut] = rows[2, cut] + fixed[2, cut] * known

            @pl.when(middle)
            def _(step=step, c=c):
                a_copy(step, c, True).start()

            @pl.when(jnp.logical_not(middle))
            def _(step=step, c=c):
                a_copy(step, c, False).start()

        if inside:
            forward(inside)

            @pl.when(jnp.logical_not(has_outer))
            def _():
                for c in early:
                    inward(c)

        xs_wait(step)
        forward(ends)
        if step == 0:
            pl.when(has_outer)(cell_loop)

        @pl.when(has_outer)
        def _():
            for c in order:
                inward(c)

        @pl.when(jnp.logical_not(has_outer))
        def _():
            for c in order[len(early):]:
                inward(c)
            if step == 0:
                cell_loop()

        for c in order:
            cut = slice(c * chunk, (c + 1) * chunk)

            @pl.when(middle)
            def _(step=step, c=c, cut=cut):
                a_copy(step, c, True).wait_recv()
                own, own_link = a_send[step, 0, cut], a_send[0, 1, cut]
                far, far_link = inner_in[step, 0, cut], inner_in[0, 1, cut]
                if step == 0:
                    fixed[6, cut] = 1.0 / (1.0 - own_link * far_link)
                rows[4, cut] = far + far_link * ((own + own_link * far) * fixed[6, cut])

            @pl.when(jnp.logical_not(middle))
            def _(step=step, c=c, cut=cut):
                b_copy(step, c).wait_recv()
                rows[4, cut] = inner_in[step, 0, cut]

            inner_value = rows[4, cut]
            outer_value = rows[3, cut] + fixed[5, cut] * inner_value
            rows[5, cut] = outer_value
            b_send[step, 0, cut] = rows[1, cut] + fixed[0, cut] * outer_value + fixed[1, cut] * inner_value

            @pl.when(has_outer)
            def _(step=step, c=c):
                b_copy(step, c).start()

        final = step == STEPS - 1

        def backward(ranges):
            lows = []
            highs = []
            for lo, hi in ranges:
                span = slice(lo, hi)
                lows.append(rows[0, span] * jnp.where(lower, rows[5, span], rows[4, span]))
                highs.append(jnp.where(lower, rows[4, span], rows[5, span]))

            def body(at, carries):
                z = m - 1 - at
                done = []
                for (lo, hi), low, later in zip(ranges, lows, carries):
                    span = slice(lo, hi)
                    solved = part[z, span] + prodr[z, span] * low + ratio[z, span] * later
                    after = solved + (source[z, span] - uptake[z, span] * solved)
                    if final:
                        out_ref[z, span] = after
                    else:
                        state[z, span] = after
                        if lo == 0:
                            edge[step + 1, 0, z] = after[0:1]
                        if hi == slab:
                            edge[step + 1, 1, z] = after[hi - lo - 1:hi - lo]
                    done.append(solved)
                return tuple(done)

            lax.fori_loop(0, m, body, tuple(highs), unroll=8)

        if final:
            backward(((0, slab),))
        else:
            backward(ends)
            xs_start(step + 1)
            if inside:
                backward(inside)

    for step in range(STEPS):
        for c in range(chunks):
            a_copy(step, c, False).wait_send()

            @pl.when(has_outer)
            def _(step=step, c=c):
                b_copy(step, c).wait_send()


def on_device(n_ax, n_xs, conc, mask, layer, stiff, prod, diff_tab, upt_tab):
    m, slab, cols = conc.shape
    chunk = 8 if slab % 8 == 0 else slab
    chunks = slab // chunk
    f32 = jnp.float32
    cells = pltpu.VMEM((m, slab, cols), f32)
    labels = pltpu.VMEM((m, slab, cols), jnp.int32)
    dma = pltpu.SemaphoreType.DMA
    vmem = lambda *shape: pltpu.VMEM(shape, f32)
    any_spec = pl.BlockSpec(memory_space=pl.ANY)
    smem_spec = pl.BlockSpec(memory_space=pltpu.SMEM)
    return pl.pallas_call(
        functools.partial(kernel, n_ax, n_xs, chunk),
        out_shape=jax.ShapeDtypeStruct((m, slab, cols), f32),
        in_specs=[any_spec] * 5 + [smem_spec] * 2,
        out_specs=pl.BlockSpec(memory_space=pltpu.VMEM),
        scratch_shapes=[
            labels, labels, cells, cells, cells, vmem(m + 2, slab, cols),
            cells, cells, cells, cells, cells, cells, cells,
            vmem(STEPS + 1, 2, m, 1, cols), vmem(STEPS + 1, 2, m, 1, cols),
            vmem(7, slab, cols), vmem(m, 1, cols),
            vmem(STEPS, 2, slab, cols), vmem(STEPS, 2, slab, cols),
            vmem(STEPS, 2, slab, cols), vmem(STEPS, 1, slab, cols), vmem(6, slab, cols),
            dma((5,)), dma((STEPS + 1, 2)), dma((STEPS + 1, 2)), dma((2,)), dma((2,)),
            dma((STEPS, chunks)), dma((STEPS, chunks)), dma((STEPS, chunks)), dma((STEPS, chunks)),
        ],
        compiler_params=pltpu.CompilerParams(
            collective_id=0, has_side_effects=True, vmem_limit_bytes=56 * 1024 * 1024
        ),
    )(conc, mask, layer, stiff, prod, diff_tab, upt_tab)


def solution(mesh):
    cells = P("ax", "xs", None)
    return jax.shard_map(
        functools.partial(on_device, mesh.shape["ax"], mesh.shape["xs"]),
        mesh=mesh, in_specs=(cells,) * 5 + (P(), P()), out_specs=cells, check_vma=False,
    )
```

```python
import functools

import jax
import jax.numpy as jnp
from jax import lax
from jax.experimental import pallas as pl
from jax.experimental.pallas import tpu as pltpu
from jax.sharding import PartitionSpec as P

STEPS = 2
RZ = 3072
SECTION_RATE = 0.05
MESH = pl.DeviceIdType.MESH


def lookup(labels, table_ref):
    summed = jnp.zeros(labels.shape, jnp.float32)
    for index in range(table_ref.shape[0]):
        summed = jnp.where(labels == index, table_ref[index], summed)
    return summed


def kernel(
    n_ax, n_xs, chunk,
    conc_hbm, mask_hbm, layer_hbm, stiff_hbm, prod_hbm, diff_tab, upt_tab,
    out_ref,
    mask, layer, stiff, source, state, root, ratio, recip, prodr, part, plane, side, uptake,
    edge, halo, fixed, shut, outer_in, inner_in, a_send, b_send, rows,
    in_sem, xs_send, xs_recv, ax_send, ax_recv, a_ssem, a_rsem, b_ssem, b_rsem,
):
    m, slab, cols = conc_hbm.shape
    chunks = slab // chunk
    me = lax.axis_index("ax")
    mx = lax.axis_index("xs")
    half = n_ax // 2
    lower = me < half
    inner = jnp.where(lower, me + 1, me - 1)
    outer = jnp.where(lower, me - 1, me + 1)
    middle = (me == half - 1) | (me == half)
    has_outer = (me > 0) & (me < n_ax - 1)

    loads = [
        pltpu.make_async_copy(src, dst, in_sem.at[at])
        for at, (src, dst) in enumerate(
            [(mask_hbm, mask), (layer_hbm, layer), (stiff_hbm, stiff), (conc_hbm, state), (prod_hbm, source)]
        )
    ]
    for load in loads:
        load.start()

    sides = (
        (mx > 0, {"xs": mx - 1}),
        (mx < n_xs - 1, {"xs": mx + 1}),
        (me > 0, {"ax": me - 1}),
        (me < n_ax - 1, {"ax": me + 1}),
    )
    barrier = pltpu.get_barrier_semaphore()
    for there, peer in sides:
        @pl.when(there)
        def _(peer=peer):
            pl.semaphore_signal(barrier, inc=1, device_id=peer, device_id_type=MESH)

    for at in range(2):
        @pl.when(jnp.logical_not(sides[at][0]))
        def _(at=at):
            for slot in range(STEPS + 1):
                halo[slot, at] = jnp.zeros((m, 1, cols), jnp.float32)

    @pl.when(jnp.logical_not(sides[2][0]))
    def _():
        root[0] = jnp.zeros((slab, cols), jnp.float32)

    @pl.when(jnp.logical_not(sides[3][0]))
    def _():
        root[m + 1] = jnp.zeros((slab, cols), jnp.float32)

    @pl.when(jnp.logical_not(has_outer))
    def _():
        for step in range(STEPS):
            for at in range(2):
                outer_in[step, at] = jnp.zeros((slab, cols), jnp.float32)

    def xs_copy(slot, at):
        return pltpu.make_async_remote_copy(
            src_ref=edge.at[slot, at], dst_ref=halo.at[slot, 1 - at],
            send_sem=xs_send.at[slot, at], recv_sem=xs_recv.at[slot, 1 - at],
            device_id=sides[at][1], device_id_type=MESH,
        )

    def xs_start(slot):
        for at in range(2):
            @pl.when(sides[at][0])
            def _(at=at):
                xs_copy(slot, at).start()

    def xs_wait(slot):
        for at in range(2):
            @pl.when(sides[at][0])
            def _(at=at):
                xs_copy(slot, 1 - at).wait_recv()
                xs_copy(slot, at).wait_send()

    def ax_copy(at):
        src, dst = ((1, m + 1), (m, 0))[at]
        return pltpu.make_async_remote_copy(
            src_ref=root.at[src], dst_ref=root.at[dst],
            send_sem=ax_send.at[at], recv_sem=ax_recv.at[1 - at],
            device_id=sides[2 + at][1], device_id_type=MESH,
        )

    def set_root(z):
        diffusivity = mask[z].astype(jnp.float32) * lookup(layer[z], diff_tab) * stiff[z]
        value = jnp.sqrt(diffusivity)
        root[z + 1] = value
        edge[STEPS, 0, z] = value[0:1]
        edge[STEPS, 1, z] = value[slab - 1:slab]

    for load in loads[:3]:
        load.wait()
    set_root(0)
    set_root(m - 1)
    pl.semaphore_wait(barrier, sum(jnp.where(there, 1, 0) for there, _ in sides))
    for at in range(2):
        @pl.when(sides[2 + at][0])
        def _(at=at):
            ax_copy(at).start()

    loads[3].wait()

    def copy_edges(z, carry):
        edge[0, 0, z] = state[z, 0:1]
        edge[0, 1, z] = state[z, slab - 1:slab]
        return carry

    lax.fori_loop(0, m, copy_edges, 0, unroll=8)
    xs_start(0)

    def root_body(z, carry):
        set_root(z)
        return carry

    lax.fori_loop(1, m - 1, root_body, 0, unroll=6)
    xs_start(STEPS)
    col_at = lax.broadcasted_iota(jnp.int32, (slab, cols), 1)

    def plane_body(z, carry):
        value = root[z + 1]
        scaled = SECTION_RATE * value
        plane[z] = scaled * pltpu.roll(value, 1, 0)
        side[z] = jnp.where(col_at == 0, 0.0, scaled * pltpu.roll(value, 1, 1))
        return carry

    lax.fori_loop(0, m, plane_body, 0, unroll=8)

    for at in range(2):
        @pl.when(sides[2 + at][0])
        def _(at=at):
            ax_copy(1 - at).wait_recv()
            ax_copy(at).wait_send()

    band_first = RZ * root[0] * root[1]
    rows[0] = band_first

    def factor_body(z, carry):
        excess, product, total = carry
        band = (RZ * root[z + 1]) * root[z + 2]
        inverse = 1.0 / (excess + band)
        ratio_now = band * inverse
        scaled = product * inverse
        ratio[z] = ratio_now
        recip[z] = inverse
        prodr[z] = scaled
        return 1.0 + ratio_now * excess, product * ratio_now, total + product * scaled

    ones = jnp.ones((slab, cols), jnp.float32)
    _, through_up, total = lax.fori_loop(0, m, factor_body, (1.0 + band_first, ones, 0.0 * ones), unroll=8)
    alpha_low = band_first * total
    alpha_high = through_up
    beta_low = band_first * prodr[m - 1]
    beta_high = ratio[m - 1]
    fixed[0] = jnp.where(lower, alpha_low, beta_high)
    fixed[1] = jnp.where(lower, alpha_high, beta_low)
    fixed[2] = jnp.where(lower, beta_low, alpha_high)
    fixed[3] = jnp.where(lower, beta_high, alpha_low)

    def fix_body(z, carry):
        scaled = SECTION_RATE * root[z + 1]
        plane[z, 0:1] = scaled[0:1] * halo[STEPS, 0, z]
        shut[z] = scaled[slab - 1:slab] * halo[STEPS, 1, z]
        return carry

    def a_copy(step, c, to_middle):
        cut = pl.ds(c * chunk, chunk)
        pick = pl.ds(0, 2 if step == 0 else 1)
        return pltpu.make_async_remote_copy(
            src_ref=a_send.at[step, pick, cut],
            dst_ref=(inner_in if to_middle else outer_in).at[step, pick, cut],
            send_sem=a_ssem.at[step, c],
            recv_sem=(b_rsem if to_middle else a_rsem).at[step, c],
            device_id={"ax": inner}, device_id_type=MESH,
        )

    def b_copy(step, c):
        cut = pl.ds(c * chunk, chunk)
        return pltpu.make_async_remote_copy(
            src_ref=b_send.at[step, 0, cut], dst_ref=inner_in.at[step, 0, cut],
            send_sem=b_ssem.at[step, c], recv_sem=b_rsem.at[step, c],
            device_id={"ax": outer}, device_id_type=MESH,
        )

    loads[4].wait()

    def cell_body(z, carry):
        weight = mask[z].astype(jnp.float32)
        uptake[z] = weight * lookup(layer[z], upt_tab)
        source[z] = weight * source[z]
        return carry

    def cell_loop():
        lax.fori_loop(0, m, cell_body, 0, unroll=8)

    if chunks > 2:
        inside = ((chunk, slab - chunk),)
        ends = ((0, chunk), (slab - chunk, slab))
        order = tuple(range(1, chunks - 1)) + (0, chunks - 1)
    else:
        inside, ends, order = (), ((0, slab),), tuple(range(chunks))
    early = order[:chunks - 2] if inside else ()

    for step in range(STEPS):

        def forward(ranges):
            def body(z, carries):
                done = []
                for (lo, hi), (moved, first) in zip(ranges, carries):
                    span = slice(lo, hi)
                    size = hi - lo
                    row = lax.broadcasted_iota(jnp.int32, (size, cols), 0)
                    now = state[z, span]
                    before = halo[step, 0, z] if lo == 0 else state[z, lo - 1:lo]
                    above = jnp.where(row == 0, before, pltpu.roll(now, 1, 0))
                    flux = plane[z, span] * (above - now)
                    if hi == slab:
                        closing = shut[z] * (now[size - 1:size] - halo[step, 1, z])
                    else:
                        closing = plane[z, hi:hi + 1] * (now[size - 1:size] - state[z, hi:hi + 1])
                    below = jnp.where(row == size - 1, closing, pltpu.roll(flux, size - 1, 0))
                    across = side[z, span] * (pltpu.roll(now, 1, 1) - now)
                    explicit = now + ((flux - below) + (across - pltpu.roll(across, cols - 1, 1)))
                    value = explicit + moved
                    part[z, span] = recip[z, span] * value
                    done.append((ratio[z, span] * value, first + prodr[z, span] * value))
                return tuple(done)

            zeros = [jnp.zeros((hi - lo, cols), jnp.float32) for lo, hi in ranges]
            sums = lax.fori_loop(0, m, body, tuple((zero, zero) for zero in zeros), unroll=8)
            for (lo, hi), (_, first) in zip(ranges, sums):
                span = slice(lo, hi)
                last = part[m - 1, span]
                rows[1, span] = jnp.where(lower, first, last)
                rows[2, span] = jnp.where(lower, last, first)

        def inward(c):
            cut = slice(c * chunk, (c + 1) * chunk)

            @pl.when(has_outer)
            def _(step=step, c=c):
                a_copy(step, c, False).wait_recv()

            link = outer_in[0, 1, cut]
            if step == 0:
                gain = 1.0 / (1.0 - link * fixed[0, cut])
                fixed[4, cut] = gain
                a_send[0, 1, cut] = fixed[3, cut] + fixed[2, cut] * (gain * link * fixed[1, cut])
                fixed[5, cut] = gain * link * fixed[1, cut]
            known = fixed[4, cut] * (outer_in[step, 0, cut] + link * rows[1, cut])
            rows[3, cut] = known
            a_send[step, 0, cut] = rows[2, cut] + fixed[2, cut] * known

            @pl.when(middle)
            def _(step=step, c=c):
                a_copy(step, c, True).start()

            @pl.when(jnp.logical_not(middle))
            def _(step=step, c=c):
                a_copy(step, c, False).start()

        if inside:
            forward(inside)

            @pl.when(jnp.logical_not(has_outer))
            def _():
                for c in early:
                    inward(c)

        if step == 0:
            xs_wait(STEPS)
            lax.fori_loop(0, m, fix_body, 0, unroll=8)
        xs_wait(step)
        forward(ends)
        if step == 0:
            pl.when(has_outer)(cell_loop)

        @pl.when(has_outer)
        def _():
            for c in order:
                inward(c)

        @pl.when(jnp.logical_not(has_outer))
        def _():
            for c in order[len(early):]:
                inward(c)
            if step == 0:
                cell_loop()

        for c in order:
            cut = slice(c * chunk, (c + 1) * chunk)

            @pl.when(middle)
            def _(step=step, c=c, cut=cut):
                a_copy(step, c, True).wait_recv()
                own, own_link = a_send[step, 0, cut], a_send[0, 1, cut]
                far, far_link = inner_in[step, 0, cut], inner_in[0, 1, cut]
                if step == 0:
                    fixed[6, cut] = 1.0 / (1.0 - own_link * far_link)
                rows[4, cut] = far + far_link * ((own + own_link * far) * fixed[6, cut])

            @pl.when(jnp.logical_not(middle))
            def _(step=step, c=c, cut=cut):
                b_copy(step, c).wait_recv()
                rows[4, cut] = inner_in[step, 0, cut]

            inner_value = rows[4, cut]
            outer_value = rows[3, cut] + fixed[5, cut] * inner_value
            rows[5, cut] = outer_value
            b_send[step, 0, cut] = rows[1, cut] + fixed[0, cut] * outer_value + fixed[1, cut] * inner_value

            @pl.when(has_outer)
            def _(step=step, c=c):
                b_copy(step, c).start()

        final = step == STEPS - 1

        def backward(ranges):
            lows = []
            highs = []
            for lo, hi in ranges:
                span = slice(lo, hi)
                lows.append(rows[0, span] * jnp.where(lower, rows[5, span], rows[4, span]))
                highs.append(jnp.where(lower, rows[4, span], rows[5, span]))

            def body(at, carries):
                z = m - 1 - at
                done = []
                for (lo, hi), low, later in zip(ranges, lows, carries):
                    span = slice(lo, hi)
                    solved = part[z, span] + prodr[z, span] * low + ratio[z, span] * later
                    after = solved + (source[z, span] - uptake[z, span] * solved)
                    if final:
                        out_ref[z, span] = after
                    else:
                        state[z, span] = after
                        if lo == 0:
                            edge[step + 1, 0, z] = after[0:1]
                        if hi == slab:
                            edge[step + 1, 1, z] = after[hi - lo - 1:hi - lo]
                    done.append(solved)
                return tuple(done)

            lax.fori_loop(0, m, body, tuple(highs), unroll=8)

        if final:
            backward(((0, slab),))
        else:
            backward(ends)
            xs_start(step + 1)
            if inside:
                backward(inside)

    for step in range(STEPS):
        for c in range(chunks):
            a_copy(step, c, False).wait_send()

            @pl.when(has_outer)
            def _(step=step, c=c):
                b_copy(step, c).wait_send()


def on_device(n_ax, n_xs, conc, mask, layer, stiff, prod, diff_tab, upt_tab):
    m, slab, cols = conc.shape
    chunk = 8 if slab % 8 == 0 else slab
    chunks = slab // chunk
    f32 = jnp.float32
    cells = pltpu.VMEM((m, slab, cols), f32)
    labels = pltpu.VMEM((m, slab, cols), jnp.int32)
    dma = pltpu.SemaphoreType.DMA
    vmem = lambda *shape: pltpu.VMEM(shape, f32)
    any_spec = pl.BlockSpec(memory_space=pl.ANY)
    smem_spec = pl.BlockSpec(memory_space=pltpu.SMEM)
    return pl.pallas_call(
        functools.partial(kernel, n_ax, n_xs, chunk),
        out_shape=jax.ShapeDtypeStruct((m, slab, cols), f32),
        in_specs=[any_spec] * 5 + [smem_spec] * 2,
        out_specs=pl.BlockSpec(memory_space=pltpu.VMEM),
        scratch_shapes=[
            labels, labels, cells, cells, cells, vmem(m + 2, slab, cols),
            cells, cells, cells, cells, cells, cells, cells,
            vmem(STEPS + 1, 2, m, 1, cols), vmem(STEPS + 1, 2, m, 1, cols),
            vmem(7, slab, cols), vmem(m, 1, cols),
            vmem(STEPS, 2, slab, cols), vmem(STEPS, 2, slab, cols),
            vmem(STEPS, 2, slab, cols), vmem(STEPS, 1, slab, cols), vmem(6, slab, cols),
            dma((5,)), dma((STEPS + 1, 2)), dma((STEPS + 1, 2)), dma((2,)), dma((2,)),
            dma((STEPS, chunks)), dma((STEPS, chunks)), dma((STEPS, chunks)), dma((STEPS, chunks)),
        ],
        compiler_params=pltpu.CompilerParams(
            collective_id=0, has_side_effects=True, vmem_limit_bytes=56 * 1024 * 1024
        ),
    )(conc, mask, layer, stiff, prod, diff_tab, upt_tab)


def solution(mesh):
    cells = P("ax", "xs", None)
    return jax.shard_map(
        functools.partial(on_device, mesh.shape["ax"], mesh.shape["xs"]),
        mesh=mesh, in_specs=(cells,) * 5 + (P(), P()), out_specs=cells, check_vma=False,
    )
```

```python
import functools

import jax
import jax.numpy as jnp
from jax import lax
from jax.experimental import pallas as pl
from jax.experimental.pallas import tpu as pltpu
from jax.sharding import PartitionSpec as P

STEPS = 2
RZ = 3072
SECTION_RATE = 0.05
MESH = pl.DeviceIdType.MESH


def lookup(labels, table_ref):
    summed = jnp.zeros(labels.shape, jnp.float32)
    for index in range(table_ref.shape[0]):
        summed = jnp.where(labels == index, table_ref[index], summed)
    return summed


def kernel(
    n_ax, n_xs, chunk,
    conc_hbm, mask_hbm, layer_hbm, stiff_hbm, prod_hbm, diff_tab, upt_tab,
    out_ref,
    mask, layer, stiff, source, state, root, ratio, recip, prodr, part, plane, side, uptake,
    edge, halo, fixed, shut, outer_in, inner_in, a_send, b_send, rows,
    in_sem, xs_send, xs_recv, ax_send, ax_recv, a_ssem, a_rsem, b_ssem, b_rsem,
):
    m, slab, cols = conc_hbm.shape
    chunks = slab // chunk
    me = lax.axis_index("ax")
    mx = lax.axis_index("xs")
    half = n_ax // 2
    lower = me < half
    inner = jnp.where(lower, me + 1, me - 1)
    outer = jnp.where(lower, me - 1, me + 1)
    middle = (me == half - 1) | (me == half)
    has_outer = (me > 0) & (me < n_ax - 1)

    loads = [
        pltpu.make_async_copy(src, dst, in_sem.at[at])
        for at, (src, dst) in enumerate(
            [(mask_hbm, mask), (layer_hbm, layer), (stiff_hbm, stiff), (conc_hbm, state), (prod_hbm, source)]
        )
    ]
    for load in loads:
        load.start()

    sides = (
        (mx > 0, {"xs": mx - 1}),
        (mx < n_xs - 1, {"xs": mx + 1}),
        (me > 0, {"ax": me - 1}),
        (me < n_ax - 1, {"ax": me + 1}),
    )
    barrier = pltpu.get_barrier_semaphore()
    for there, peer in sides:
        @pl.when(there)
        def _(peer=peer):
            pl.semaphore_signal(barrier, inc=1, device_id=peer, device_id_type=MESH)

    for at in range(2):
        @pl.when(jnp.logical_not(sides[at][0]))
        def _(at=at):
            for slot in range(STEPS + 1):
                halo[slot, at] = jnp.zeros((m, 1, cols), jnp.float32)

    @pl.when(jnp.logical_not(sides[2][0]))
    def _():
        root[0] = jnp.zeros((slab, cols), jnp.float32)

    @pl.when(jnp.logical_not(sides[3][0]))
    def _():
        root[m + 1] = jnp.zeros((slab, cols), jnp.float32)

    @pl.when(jnp.logical_not(has_outer))
    def _():
        for step in range(STEPS):
            for at in range(2):
                outer_in[step, at] = jnp.zeros((slab, cols), jnp.float32)

    def xs_copy(slot, at):
        return pltpu.make_async_remote_copy(
            src_ref=edge.at[slot, at], dst_ref=halo.at[slot, 1 - at],
            send_sem=xs_send.at[slot, at], recv_sem=xs_recv.at[slot, 1 - at],
            device_id=sides[at][1], device_id_type=MESH,
        )

    def xs_start(slot):
        for at in range(2):
            @pl.when(sides[at][0])
            def _(at=at):
                xs_copy(slot, at).start()

    def xs_wait(slot):
        for at in range(2):
            @pl.when(sides[at][0])
            def _(at=at):
                xs_copy(slot, 1 - at).wait_recv()
                xs_copy(slot, at).wait_send()

    def ax_copy(at):
        src, dst = ((1, m + 1), (m, 0))[at]
        return pltpu.make_async_remote_copy(
            src_ref=root.at[src], dst_ref=root.at[dst],
            send_sem=ax_send.at[at], recv_sem=ax_recv.at[1 - at],
            device_id=sides[2 + at][1], device_id_type=MESH,
        )

    def set_root(z):
        diffusivity = mask[z].astype(jnp.float32) * lookup(layer[z], diff_tab) * stiff[z]
        value = jnp.sqrt(diffusivity)
        root[z + 1] = value
        edge[STEPS, 0, z] = value[0:1]
        edge[STEPS, 1, z] = value[slab - 1:slab]

    for load in loads[:3]:
        load.wait()
    set_root(0)
    set_root(m - 1)
    pl.semaphore_wait(barrier, sum(jnp.where(there, 1, 0) for there, _ in sides))
    for at in range(2):
        @pl.when(sides[2 + at][0])
        def _(at=at):
            ax_copy(at).start()

    loads[3].wait()

    def copy_edges(z, carry):
        edge[0, 0, z] = state[z, 0:1]
        edge[0, 1, z] = state[z, slab - 1:slab]
        return carry

    lax.fori_loop(0, m, copy_edges, 0, unroll=16)
    xs_start(0)

    def root_body(z, carry):
        set_root(z)
        return carry

    lax.fori_loop(1, m - 1, root_body, 0, unroll=6)
    xs_start(STEPS)
    col_at = lax.broadcasted_iota(jnp.int32, (slab, cols), 1)

    def plane_body(z, carry):
        value = root[z + 1]
        scaled = SECTION_RATE * value
        plane[z] = scaled * pltpu.roll(value, 1, 0)
        side[z] = jnp.where(col_at == 0, 0.0, scaled * pltpu.roll(value, 1, 1))
        return carry

    lax.fori_loop(0, m, plane_body, 0, unroll=16)

    for at in range(2):
        @pl.when(sides[2 + at][0])
        def _(at=at):
            ax_copy(1 - at).wait_recv()
            ax_copy(at).wait_send()

    band_first = RZ * root[0] * root[1]
    rows[0] = band_first

    def factor_body(z, carry):
        excess, product, total = carry
        band = (RZ * root[z + 1]) * root[z + 2]
        inverse = 1.0 / (excess + band)
        ratio_now = band * inverse
        scaled = product * inverse
        ratio[z] = ratio_now
        recip[z] = inverse
        prodr[z] = scaled
        return 1.0 + ratio_now * excess, product * ratio_now, total + product * scaled

    ones = jnp.ones((slab, cols), jnp.float32)
    _, through_up, total = lax.fori_loop(0, m, factor_body, (1.0 + band_first, ones, 0.0 * ones), unroll=16)
    alpha_low = band_first * total
    alpha_high = through_up
    beta_low = band_first * prodr[m - 1]
    beta_high = ratio[m - 1]
    fixed[0] = jnp.where(lower, alpha_low, beta_high)
    fixed[1] = jnp.where(lower, alpha_high, beta_low)
    fixed[2] = jnp.where(lower, beta_low, alpha_high)
    fixed[3] = jnp.where(lower, beta_high, alpha_low)

    def fix_body(z, carry):
        scaled = SECTION_RATE * root[z + 1]
        plane[z, 0:1] = scaled[0:1] * halo[STEPS, 0, z]
        shut[z] = scaled[slab - 1:slab] * halo[STEPS, 1, z]
        return carry

    def a_copy(step, c, to_middle):
        cut = pl.ds(c * chunk, chunk)
        pick = pl.ds(0, 2 if step == 0 else 1)
        return pltpu.make_async_remote_copy(
            src_ref=a_send.at[step, pick, cut],
            dst_ref=(inner_in if to_middle else outer_in).at[step, pick, cut],
            send_sem=a_ssem.at[step, c],
            recv_sem=(b_rsem if to_middle else a_rsem).at[step, c],
            device_id={"ax": inner}, device_id_type=MESH,
        )

    def b_copy(step, c):
        cut = pl.ds(c * chunk, chunk)
        return pltpu.make_async_remote_copy(
            src_ref=b_send.at[step, 0, cut], dst_ref=inner_in.at[step, 0, cut],
            send_sem=b_ssem.at[step, c], recv_sem=b_rsem.at[step, c],
            device_id={"ax": outer}, device_id_type=MESH,
        )

    loads[4].wait()

    def cell_body(z, carry):
        weight = mask[z].astype(jnp.float32)
        uptake[z] = weight * lookup(layer[z], upt_tab)
        source[z] = weight * source[z]
        return carry

    def cell_loop():
        lax.fori_loop(0, m, cell_body, 0, unroll=16)

    if chunks > 2:
        inside = ((chunk, slab - chunk),)
        ends = ((0, chunk), (slab - chunk, slab))
        order = tuple(range(1, chunks - 1)) + (0, chunks - 1)
    else:
        inside, ends, order = (), ((0, slab),), tuple(range(chunks))
    early = order[:chunks - 2] if inside else ()

    for step in range(STEPS):

        def forward(ranges):
            def body(z, carries):
                done = []
                for (lo, hi), (moved, first) in zip(ranges, carries):
                    span = slice(lo, hi)
                    size = hi - lo
                    row = lax.broadcasted_iota(jnp.int32, (size, cols), 0)
                    now = state[z, span]
                    before = halo[step, 0, z] if lo == 0 else state[z, lo - 1:lo]
                    above = jnp.where(row == 0, before, pltpu.roll(now, 1, 0))
                    flux = plane[z, span] * (above - now)
                    if hi == slab:
                        closing = shut[z] * (now[size - 1:size] - halo[step, 1, z])
                    else:
                        closing = plane[z, hi:hi + 1] * (now[size - 1:size] - state[z, hi:hi + 1])
                    below = jnp.where(row == size - 1, closing, pltpu.roll(flux, size - 1, 0))
                    across = side[z, span] * (pltpu.roll(now, 1, 1) - now)
                    explicit = now + ((flux - below) + (across - pltpu.roll(across, cols - 1, 1)))
                    value = explicit + moved
                    part[z, span] = recip[z, span] * value
                    done.append((ratio[z, span] * value, first + prodr[z, span] * value))
                return tuple(done)

            zeros = [jnp.zeros((hi - lo, cols), jnp.float32) for lo, hi in ranges]
            sums = lax.fori_loop(0, m, body, tuple((zero, zero) for zero in zeros), unroll=16)
            for (lo, hi), (_, first) in zip(ranges, sums):
                span = slice(lo, hi)
                last = part[m - 1, span]
                rows[1, span] = jnp.where(lower, first, last)
                rows[2, span] = jnp.where(lower, last, first)

        def inward(c):
            cut = slice(c * chunk, (c + 1) * chunk)

            @pl.when(has_outer)
            def _(step=step, c=c):
                a_copy(step, c, False).wait_recv()

            link = outer_in[0, 1, cut]
            if step == 0:
                gain = 1.0 / (1.0 - link * fixed[0, cut])
                fixed[4, cut] = gain
                a_send[0, 1, cut] = fixed[3, cut] + fixed[2, cut] * (gain * link * fixed[1, cut])
                fixed[5, cut] = gain * link * fixed[1, cut]
            known = fixed[4, cut] * (outer_in[step, 0, cut] + link * rows[1, cut])
            rows[3, cut] = known
            a_send[step, 0, cut] = rows[2, cut] + fixed[2, cut] * known

            @pl.when(middle)
            def _(step=step, c=c):
                a_copy(step, c, True).start()

            @pl.when(jnp.logical_not(middle))
            def _(step=step, c=c):
                a_copy(step, c, False).start()

        if inside:
            forward(inside)

            @pl.when(jnp.logical_not(has_outer))
            def _():
                for c in early:
                    inward(c)

        if step == 0:
            xs_wait(STEPS)
            lax.fori_loop(0, m, fix_body, 0, unroll=16)
        xs_wait(step)
        forward(ends)
        if step == 0:
            pl.when(has_outer)(cell_loop)

        @pl.when(has_outer)
        def _():
            for c in order:
                inward(c)

        @pl.when(jnp.logical_not(has_outer))
        def _():
            for c in order[len(early):]:
                inward(c)
            if step == 0:
                cell_loop()

        for c in order:
            cut = slice(c * chunk, (c + 1) * chunk)

            @pl.when(middle)
            def _(step=step, c=c, cut=cut):
                a_copy(step, c, True).wait_recv()
                own, own_link = a_send[step, 0, cut], a_send[0, 1, cut]
                far, far_link = inner_in[step, 0, cut], inner_in[0, 1, cut]
                if step == 0:
                    fixed[6, cut] = 1.0 / (1.0 - own_link * far_link)
                rows[4, cut] = far + far_link * ((own + own_link * far) * fixed[6, cut])

            @pl.when(jnp.logical_not(middle))
            def _(step=step, c=c, cut=cut):
                b_copy(step, c).wait_recv()
                rows[4, cut] = inner_in[step, 0, cut]

            inner_value = rows[4, cut]
            outer_value = rows[3, cut] + fixed[5, cut] * inner_value
            rows[5, cut] = outer_value
            b_send[step, 0, cut] = rows[1, cut] + fixed[0, cut] * outer_value + fixed[1, cut] * inner_value

            @pl.when(has_outer)
            def _(step=step, c=c):
                b_copy(step, c).start()

        final = step == STEPS - 1

        def backward(ranges):
            lows = []
            highs = []
            for lo, hi in ranges:
                span = slice(lo, hi)
                lows.append(rows[0, span] * jnp.where(lower, rows[5, span], rows[4, span]))
                highs.append(jnp.where(lower, rows[4, span], rows[5, span]))

            def body(at, carries):
                z = m - 1 - at
                done = []
                for (lo, hi), low, later in zip(ranges, lows, carries):
                    span = slice(lo, hi)
                    solved = part[z, span] + prodr[z, span] * low + ratio[z, span] * later
                    after = solved + (source[z, span] - uptake[z, span] * solved)
                    if final:
                        out_ref[z, span] = after
                    else:
                        state[z, span] = after
                        if lo == 0:
                            edge[step + 1, 0, z] = after[0:1]
                        if hi == slab:
                            edge[step + 1, 1, z] = after[hi - lo - 1:hi - lo]
                    done.append(solved)
                return tuple(done)

            lax.fori_loop(0, m, body, tuple(highs), unroll=16)

        if final:
            backward(((0, slab),))
        else:
            backward(ends)
            xs_start(step + 1)
            if inside:
                backward(inside)

    for step in range(STEPS):
        for c in range(chunks):
            a_copy(step, c, False).wait_send()

            @pl.when(has_outer)
            def _(step=step, c=c):
                b_copy(step, c).wait_send()


def on_device(n_ax, n_xs, conc, mask, layer, stiff, prod, diff_tab, upt_tab):
    m, slab, cols = conc.shape
    chunk = 8 if slab % 8 == 0 else slab
    chunks = slab // chunk
    f32 = jnp.float32
    cells = pltpu.VMEM((m, slab, cols), f32)
    labels = pltpu.VMEM((m, slab, cols), jnp.int32)
    dma = pltpu.SemaphoreType.DMA
    vmem = lambda *shape: pltpu.VMEM(shape, f32)
    any_spec = pl.BlockSpec(memory_space=pl.ANY)
    smem_spec = pl.BlockSpec(memory_space=pltpu.SMEM)
    return pl.pallas_call(
        functools.partial(kernel, n_ax, n_xs, chunk),
        out_shape=jax.ShapeDtypeStruct((m, slab, cols), f32),
        in_specs=[any_spec] * 5 + [smem_spec] * 2,
        out_specs=pl.BlockSpec(memory_space=pltpu.VMEM),
        scratch_shapes=[
            labels, labels, cells, cells, cells, vmem(m + 2, slab, cols),
            cells, cells, cells, cells, cells, cells, cells,
            vmem(STEPS + 1, 2, m, 1, cols), vmem(STEPS + 1, 2, m, 1, cols),
            vmem(7, slab, cols), vmem(m, 1, cols),
            vmem(STEPS, 2, slab, cols), vmem(STEPS, 2, slab, cols),
            vmem(STEPS, 2, slab, cols), vmem(STEPS, 1, slab, cols), vmem(6, slab, cols),
            dma((5,)), dma((STEPS + 1, 2)), dma((STEPS + 1, 2)), dma((2,)), dma((2,)),
            dma((STEPS, chunks)), dma((STEPS, chunks)), dma((STEPS, chunks)), dma((STEPS, chunks)),
        ],
        compiler_params=pltpu.CompilerParams(
            collective_id=0, has_side_effects=True, vmem_limit_bytes=56 * 1024 * 1024
        ),
    )(conc, mask, layer, stiff, prod, diff_tab, upt_tab)


def solution(mesh):
    cells = P("ax", "xs", None)
    return jax.shard_map(
        functools.partial(on_device, mesh.shape["ax"], mesh.shape["xs"]),
        mesh=mesh, in_specs=(cells,) * 5 + (P(), P()), out_specs=cells, check_vma=False,
    )
```
